32 devices in a mesh: band: 8 (over z, y), head: 4 (over x, core).
Axes of the slice: x: 2, y: 2, z: 4, core: 2. Of those that a mesh axis runs over, the one named last changes fastest.
Arguments:
- grid_feat: bfloat16 [65536, 1024], P(('band', 'head')), may hold values from -7 to 7
- mesh_feat: bfloat16 [4096, 1024], P(('band', 'head')), may hold values from -7 to 7
- enc_query: bfloat16 [1024, 1024], replicated, may hold values from -0.1875 to 0.1875
- enc_keyval: bfloat16 [1024, 2048], replicated, may hold values from -0.1875 to 0.1875
- enc_out: bfloat16 [1024, 1024], replicated, may hold values from -0.1875 to 0.1875
- proc_qkv: bfloat16 [3, 1024, 1024], P(None, None, 'head'), may hold values from -0.1875 to 0.1875
- proc_out: bfloat16 [1024, 1024], P('head'), may hold values from -0.1875 to 0.1875
- tile_ids: int32 [64, 8], P(('band', 'head')), may hold values from 0 to 511, as said below
- key_counts: int32 [64], P(('band', 'head')), may hold values from 128 to 1024, as said below
Outputs:
- mesh_out: bfloat16 [4096, 1024], P(('band', 'head'))
The draws below stay inside these ranges and needn't reach their ends.
Inputs may be any that keep to these rules, and one draw needn't show every extreme that they name: `tile_ids`: mesh tile m lies on the device that holds mesh rows m * 64; every tile it lists is one of that device's grid tiles (grid rows of the same device) or of the 2 grid tiles just before or just after them. Slots may repeat tiles. `key_counts`: the largest value is reached in every draw.
All inputs are finite; a program needn't handle non-finite values.
Results may differ from the reference program's by a relative error of at most 0.012.
The reference program's roundings to bfloat16 on the way count: a program that leaves them out, or rounds other values in their place, can miss the bound.
Values may be sent and summed in bfloat16 or wider, within the bound.
A program may use at most 128 MiB of HBM per device.

```python
import math
import jax
import jax.numpy as jnp
from jax import lax

D = 1024
HEADS = 16
HALFW = 512
GT = 128
LIST = 8
MT = 64
HALO_TILES = 2
GRID_DEV = 2048
MESH_DEV = 128
GRID = 65536
MESH = 4096


def feature_draw(key, row_count):
    values = jnp.clip(jax.random.normal(key, (row_count, D), jnp.float32), -5.0, 5.0)
    return values.astype(jnp.bfloat16)


def draw_grid_feat(key, part):
    return feature_draw(jax.random.fold_in(key, 11), GRID)


def draw_mesh_feat(key, part):
    return feature_draw(jax.random.fold_in(key, 12), MESH)


def draw_tile_ids(key, part):
    tiles_mesh = MESH // MT
    per_device = MESH_DEV // MT
    tiles_device = GRID_DEV // GT
    owner = jnp.arange(tiles_mesh, dtype=jnp.int32) // per_device
    first_tile = owner * tiles_device - HALO_TILES
    offsets = jax.random.randint(jax.random.fold_in(key, 21), (tiles_mesh, LIST), 0, tiles_device + 2 * HALO_TILES)
    return jnp.clip(first_tile[:, None] + offsets, 0, GRID // GT - 1).astype(jnp.int32)


def draw_key_counts(key, part):
    tiles_mesh = MESH // MT
    counts = jax.random.randint(jax.random.fold_in(key, 31), (tiles_mesh,), GT, LIST * GT + 1)
    position = jax.random.randint(jax.random.fold_in(key, 32), (), 0, tiles_mesh)
    return counts.at[position].set(LIST * GT).astype(jnp.int32)


def block_levels(key, shape, pieces, smallest, largest):
    def one(dim, shards_of):
        heights = jax.random.uniform(jax.random.fold_in(jax.random.fold_in(key, 6), dim), (shards_of,), jnp.float32, smallest / len(pieces), largest / len(pieces))
        return jnp.repeat(jnp.exp(heights), shape[dim] // shards_of).reshape((-1,) + (1,) * (len(shape) - dim - 1))

    level = one(*pieces[0])
    for cut in pieces[1:]:
        level = level * one(*cut)
    return level


def bell_draw(own_key, shape, scale, reach, cuts=(), kind=jnp.bfloat16):
    values = jax.random.normal(own_key, shape, jnp.float32) * scale
    if len(cuts) > 0:
        values = block_levels(own_key, shape, cuts, -0.22, 0.18) * values
    return jnp.clip(values, min=-reach, max=reach).astype(kind)


def setup_inputs(seed: int = 0) -> dict:
    key_of = jax.random.split(jax.random.key(seed), 10)
    grid_feat = draw_grid_feat(jax.random.fold_in(key_of[9], 71), 0)
    mesh_feat = draw_mesh_feat(jax.random.fold_in(key_of[9], 71), 0)
    enc_query = bell_draw(key_of[2], (D, D), D ** -0.5, 0.1875)
    enc_keyval = bell_draw(key_of[3], (D, 2 * D), D ** -0.5, 0.1875)
    enc_out = bell_draw(key_of[4], (D, D), D ** -0.5, 0.1875)
    proc_qkv = bell_draw(key_of[5], (3, D, D), D ** -0.5, 0.1875, ((2, 4),))
    proc_out = bell_draw(key_of[6], (D, D), D ** -0.5, 0.1875, ((0, 4),))
    tile_ids = draw_tile_ids(jax.random.fold_in(key_of[9], 71), 0)
    key_counts = draw_key_counts(jax.random.fold_in(key_of[9], 71), 0)
    return {"grid_feat": grid_feat, "mesh_feat": mesh_feat, "enc_query": enc_query, "enc_keyval": enc_keyval, "enc_out": enc_out, "proc_qkv": proc_qkv, "proc_out": proc_out, "tile_ids": tile_ids, "key_counts": key_counts}


def masked_softmax(scores, key_mask):
    scores = jnp.where(key_mask, scores, -1e30)
    row_top = jnp.max(scores, axis=-1, keepdims=True)
    weights = jnp.exp(scores - row_top)
    return (weights / jnp.sum(weights, axis=-1, keepdims=True)).astype(jnp.bfloat16)


def reference(grid_feat, mesh_feat, enc_query, enc_keyval, enc_out, proc_qkv, proc_out, tile_ids, key_counts):
    head_size = D // HEADS
    score_scale = head_size ** -0.5
    grid_kv = jnp.dot(grid_feat, enc_keyval, preferred_element_type=jnp.float32).astype(jnp.bfloat16)
    grid_tiles = grid_kv.reshape(GRID // GT, GT, 2 * D)
    queries = jnp.dot(mesh_feat, enc_query, preferred_element_type=jnp.float32).astype(jnp.bfloat16)
    positions = jnp.arange(LIST * GT, dtype=jnp.int32)

    def one_tile(packed):
        query_tile, tile_list, valid = packed
        gathered = grid_tiles[tile_list].reshape(LIST * GT, 2 * D)
        key_rows = gathered[:, :D].reshape(LIST * GT, HEADS, head_size).astype(jnp.float32)
        value_rows = gathered[:, D:].reshape(LIST * GT, HEADS, head_size).astype(jnp.float32)
        query_heads = query_tile.reshape(MT, HEADS, head_size).astype(jnp.float32)
        scores = jnp.einsum("qhd,khd->hqk", query_heads, key_rows) * score_scale
        weights = masked_softmax(scores, (positions < valid)[None, None, :])
        attended = jnp.einsum("hqk,khd->qhd", weights.astype(jnp.float32), value_rows)
        return attended.reshape(MT, D).astype(jnp.bfloat16)

    enc_attn = lax.map(one_tile, (queries.reshape(MESH // MT, MT, D), tile_ids, key_counts)).reshape(MESH, D)
    mesh_state = (mesh_feat.astype(jnp.float32) + jnp.dot(enc_attn, enc_out, preferred_element_type=jnp.float32)).astype(jnp.bfloat16)
    query_all = jnp.dot(mesh_state, proc_qkv[0], preferred_element_type=jnp.float32).astype(jnp.bfloat16)
    key_all = jnp.dot(mesh_state, proc_qkv[1], preferred_element_type=jnp.float32).astype(jnp.bfloat16)
    value_all = jnp.dot(mesh_state, proc_qkv[2], preferred_element_type=jnp.float32).astype(jnp.bfloat16)
    padded_keys = jnp.pad(key_all, ((HALFW, HALFW), (0, 0)))
    padded_values = jnp.pad(value_all, ((HALFW, HALFW), (0, 0)))
    block_rows = math.gcd(MESH, 512)

    def one_block(block_index):
        first = block_index * block_rows
        span = block_rows + 2 * HALFW
        query_heads = lax.dynamic_slice_in_dim(query_all, first, block_rows, 0).reshape(block_rows, HEADS, head_size).astype(jnp.float32)
        key_rows = lax.dynamic_slice_in_dim(padded_keys, first, span, 0).reshape(span, HEADS, head_size).astype(jnp.float32)
        value_rows = lax.dynamic_slice_in_dim(padded_values, first, span, 0).reshape(span, HEADS, head_size).astype(jnp.float32)
        query_pos = first + jnp.arange(block_rows, dtype=jnp.int32)
        key_pos = first - HALFW + jnp.arange(span, dtype=jnp.int32)
        near = (jnp.abs(query_pos[:, None] - key_pos[None, :]) < HALFW) & ((key_pos >= 0) & (key_pos < MESH))[None, :]
        scores = jnp.einsum("qhd,khd->hqk", query_heads, key_rows) * score_scale
        weights = masked_softmax(scores, near[None, :, :])
        attended = jnp.einsum("hqk,khd->qhd", weights.astype(jnp.float32), value_rows)
        return attended.reshape(block_rows, D).astype(jnp.bfloat16)

    proc_attn = lax.map(one_block, jnp.arange(MESH // block_rows, dtype=jnp.int32)).reshape(MESH, D)
    return (mesh_state.astype(jnp.float32) + jnp.dot(proc_attn, proc_out, preferred_element_type=jnp.float32)).astype(jnp.bfloat16)
```

```python
import functools

import jax
import jax.numpy as jnp
from jax import lax
from jax.experimental import pallas as pl
from jax.experimental.pallas import tpu as pltpu
from jax.sharding import PartitionSpec as P

HEADS = 16
HALFW = 512
GT = 128
MT = 64
HALO_TILES = 2
BF = jnp.bfloat16
F32 = jnp.float32
MESH_ID = pl.DeviceIdType.MESH
NEG = -1e30


def dot(a, b):
    return jnp.dot(a, b, preferred_element_type=F32)


def dot_t(a, b):
    return lax.dot_general(a, b, (((1,), (1,)), ((), ())), preferred_element_type=F32)


def pair_rows(q2, half):
    lane = lax.broadcasted_iota(jnp.int32, q2.shape, 1)
    low = lane < half
    zero = jnp.zeros_like(q2)
    return jnp.concatenate([jnp.where(low, q2, zero), jnp.where(low, zero, q2)], axis=0)


def pair_merge(o2, rows, half):
    lane = lax.broadcasted_iota(jnp.int32, (rows, 2 * half), 1)
    return jnp.where(lane < half, o2[:rows], o2[rows:])


def softmax_rows(scores):
    top = jnp.max(scores, axis=-1, keepdims=True)
    weights = jnp.exp(scores - top)
    return (weights * (1.0 / jnp.sum(weights, axis=-1, keepdims=True))).astype(BF)


def kernel(
    nb, nh, tid, cnt, grid, feat_h, wquery_h, wkv_h, wenc_h, qkv_h, pout_h, out,
    g, halo, wkv, wquery, wenc, feat, kv, wq, wo, st, qs, att, kp, vp, bias,
    lsem, hs_send, hs_recv,
    wp_send, wp_recv, wx_send, wx_recv, wy_send, wy_recv, wf_send, wf_recv, wg_send, wg_recv,
    s_send, s_recv, f_send,
):
    n = nb * nh
    band = lax.axis_index("band")
    head = lax.axis_index("head")
    d = band * nh + head
    core = lax.rem(head, 2)
    par = lax.rem(band, 2)
    mate = head + 1 - 2 * core
    twin = band + 1 - 2 * par
    xs = nh // 2
    rows, dm = feat.shape
    tiles = grid.shape[0] // GT
    edge = HALO_TILES * GT
    cols = qkv_h.shape[2]
    slots = st.shape[0]
    reach = slots // 2
    head_size = dm // HEADS
    pairs = HEADS // 2
    wide = 2 * head_size
    scale = head_size ** (-0.5)

    def flat_id(f):
        return (f // nh, lax.rem(f, nh))

    def remote(src, dst, ss, rs, dev):
        return pltpu.make_async_remote_copy(
            src_ref=src, dst_ref=dst, send_sem=ss, recv_sem=rs, device_id=dev,
            device_id_type=MESH_ID)

    gchunk = g.shape[0] // 4
    wchunk = wkv.shape[1] // 4
    local = []
    for i in range(4):
        local.append(pltpu.make_async_copy(
            wkv_h.at[:, pl.ds(i * wchunk, wchunk)], wkv.at[:, pl.ds(i * wchunk, wchunk)],
            lsem.at[i]))
        local.append(pltpu.make_async_copy(
            grid.at[pl.ds(i * gchunk, gchunk)], g.at[pl.ds(i * gchunk, gchunk)], lsem.at[4 + i]))
    local.append(pltpu.make_async_copy(feat_h, feat, lsem.at[8]))
    local.append(pltpu.make_async_copy(wquery_h, wquery, lsem.at[9]))
    local.append(pltpu.make_async_copy(wenc_h, wenc, lsem.at[10]))
    local.append(pltpu.make_async_copy(qkv_h, wq.at[head], lsem.at[11]))
    own_out = pl.multiple_of(head * cols, cols)
    local.append(pltpu.make_async_copy(pout_h, wo.at[pl.ds(own_out, cols)], lsem.at[12]))
    for c in local:
        c.start()

    bar = pltpu.get_barrier_semaphore()
    expect = jnp.int32(0)
    for off in (-4, -2, -1, 1, 2, 4):
        ok = (d + off >= 0) & (d + off < n)
        expect = expect + ok.astype(jnp.int32)

        @pl.when(ok)
        def _(off=off):
            pl.semaphore_signal(bar, inc=1, device_id=flat_id(d + off), device_id_type=MESH_ID)

    for k in range(1, xs):
        pl.semaphore_signal(bar, inc=1, device_id=(band, lax.rem(head + 2 * k, nh)),
                            device_id_type=MESH_ID)
    pl.semaphore_signal(bar, inc=1, device_id=(twin, head), device_id_type=MESH_ID)
    pl.semaphore_signal(bar, inc=1, device_id=(band, mate), device_id_type=MESH_ID)
    pl.semaphore_wait(bar, expect + (xs + 1))

    first, last = d == 0, d == n - 1
    up = remote(grid.at[pl.ds(grid.shape[0] - edge, edge)], halo.at[0], hs_send.at[0],
                hs_recv.at[0], flat_id(lax.rem(d + 1, n)))
    down = remote(grid.at[pl.ds(0, edge)], halo.at[1], hs_send.at[1], hs_recv.at[1],
                  flat_id(lax.rem(d + n - 1, n)))

    @pl.when(jnp.logical_not(last))
    def _():
        up.start()

    @pl.when(jnp.logical_not(first))
    def _():
        down.start()

    @pl.when(first)
    def _():
        halo[0] = jnp.zeros(halo.shape[1:], BF)

    @pl.when(last)
    def _():
        halo[1] = jnp.zeros(halo.shape[1:], BF)

    half = dm // 2
    ohalf = cols // 2

    def piece(p, src, y):
        if p < 3:
            t = (1, 2, 0)[p]
            return wq.at[src, t, pl.ds(pl.multiple_of(y * half, half), half)]
        return wo.at[pl.ds(pl.multiple_of(src * cols + y * ohalf, ohalf), ohalf)]

    def own_piece(p, y):
        if p < 3:
            t = (1, 2, 0)[p]
            return qkv_h.at[t, pl.ds(pl.multiple_of(y * half, half), half)]
        return pout_h.at[pl.ds(pl.multiple_of(y * ohalf, ohalf), ohalf)]

    def full_piece(p, src):
        if p < 3:
            return wq.at[src, (1, 2, 0)[p]]
        return wo.at[pl.ds(pl.multiple_of(src * cols, cols), cols)]

    def own_full(p):
        return qkv_h.at[(1, 2, 0)[p]] if p < 3 else pout_h

    def src_of(h, k):
        return lax.rem(h - 2 * k + nh, nh)

    def cross(p, k):
        return remote(own_piece(p, par), piece(p, head, par), wx_send.at[p, k - 1],
                      wx_recv.at[p, k - 1], (band, lax.rem(head + 2 * k, nh)))

    def to_mate(p):
        return remote(own_full(p), full_piece(p, head), wp_send.at[p], wp_recv.at[p], (band, mate))

    def relay(p, k, y, ss, rs, dev):
        src = src_of(head, k)
        return remote(piece(p, src, y), piece(p, src, y), ss.at[p, k - 1], rs.at[p, k - 1], dev)

    def to_twin(p, k):
        return relay(p, k, par, wy_send, wy_recv, (twin, head))

    def near_mate(p, k):
        return relay(p, k, par, wf_send, wf_recv, (band, mate))

    def far_mate(p, k):
        return relay(p, k, 1 - par, wg_send, wg_recv, (band, mate))

    for p in range(4):
        for k in range(1, xs):
            cross(p, k).start()
        to_mate(p).start()

    def stage_one(p):
        for k in range(1, xs):
            src = src_of(head, k)
            remote(own_piece(p, par), piece(p, src, par), wx_send.at[p, k - 1],
                   wx_recv.at[p, k - 1], (band, mate)).wait_recv()
            to_twin(p, k).start()
            near_mate(p, k).start()

    def stage_two(p):
        for k in range(1, xs):
            src = src_of(head, k)
            remote(own_piece(p, par), piece(p, src, 1 - par), wy_send.at[p, k - 1],
                   wy_recv.at[p, k - 1], (band, mate)).wait_recv()
            far_mate(p, k).start()

    def stage_three(p):
        remote(own_full(p), full_piece(p, mate), wp_send.at[p], wp_recv.at[p],
               (band, mate)).wait_recv()
        for k in range(1, xs):
            src = src_of(mate, k)
            for y, ss, rs in ((par, wf_send, wf_recv), (1 - par, wg_send, wg_recv)):
                remote(own_piece(p, y), piece(p, src, y), ss.at[p, k - 1], rs.at[p, k - 1],
                       (band, mate)).wait_recv()

    for e in range(slots):
        if e != reach:
            ok = (d - reach + e >= 0) & (d - reach + e < n)

            @pl.when(jnp.logical_not(ok))
            def _(e=e):
                st[e] = jnp.zeros(st.shape[1:], BF)

    brow = lax.broadcasted_iota(jnp.int32, (rows, slots * rows), 0)
    bcol = lax.broadcasted_iota(jnp.int32, (rows, slots * rows), 1)
    kpos = (d - reach) * rows + bcol
    near = (bcol - HALFW - brow < HALFW) & (bcol - HALFW - brow > -HALFW)
    near = near & (kpos >= 0) & (kpos < n * rows)
    bias[...] = jnp.where(near, 0.0, NEG).astype(F32)

    for i in range(4):
        local[2 * i].wait()
    for i in range(4):
        local[2 * i + 1].wait()
        ct = gchunk // GT

        def col_step(j, _, i=i, ct=ct):
            cs = pl.ds(pl.multiple_of(j * wchunk, wchunk), wchunk)
            r = dot(g[pl.ds(i * gchunk, gchunk)], wkv[:, cs]).astype(BF)
            kv[pl.ds(HALO_TILES + i * ct, ct), :, cs] = r.reshape(ct, GT, wchunk)
            return 0

        lax.fori_loop(0, 4, col_step, 0)
    local[8].wait()
    local[9].wait()
    local[10].wait()
    qs[...] = (dot(feat[...], wquery[...]).astype(BF) * scale).astype(BF)

    @pl.when(jnp.logical_not(first))
    def _():
        up.wait_recv()

    @pl.when(jnp.logical_not(last))
    def _():
        down.wait_recv()

    def halo_step(j, _):
        cs = pl.ds(pl.multiple_of(j * wchunk, wchunk), wchunk)
        r = dot(halo[...].reshape(2 * edge, dm), wkv[:, cs]).astype(BF)
        r = r.reshape(2 * HALO_TILES, GT, wchunk)
        kv[pl.ds(0, HALO_TILES), :, cs] = r[:HALO_TILES]
        kv[pl.ds(HALO_TILES + tiles, HALO_TILES), :, cs] = r[HALO_TILES:]
        return 0

    lax.fori_loop(0, 4, halo_step, 0)
    stage_one(0)

    base = d * tiles - HALO_TILES
    lists = tid.shape[1]
    for m in range(rows // MT):
        ids = [jnp.clip(tid[m, s] - base, 0, kv.shape[0] - 1) for s in range(lists)]
        valid = cnt[m]

        def pair_step(j, _, m=m, ids=ids, valid=valid):
            cs = pl.ds(pl.multiple_of(j * wide, wide), wide)
            vs = pl.ds(pl.multiple_of(dm + j * wide, wide), wide)
            q2 = pair_rows(qs[pl.ds(m * MT, MT), cs], head_size)
            k2 = jnp.concatenate([kv[t, :, cs] for t in ids], axis=0)
            scores = dot_t(q2, k2)
            pos = lax.broadcasted_iota(jnp.int32, scores.shape, 1)
            w = softmax_rows(jnp.where(pos < valid, scores, NEG))
            v2 = jnp.concatenate([kv[t, :, vs] for t in ids], axis=0)
            att[pl.ds(m * MT, MT), cs] = pair_merge(dot(w, v2), MT, head_size).astype(BF)
            return 0

        lax.fori_loop(0, pairs, pair_step, 0)
        if m == 0:
            stage_one(1)
    st[reach] = (feat[...].astype(F32) + dot(att[...], wenc[...])).astype(BF)

    mate_slot = reach + 1 - 2 * core

    def state_to(i, off):
        return remote(st.at[reach], st.at[reach - off], s_send.at[i], s_recv.at[reach - off],
                      flat_id(lax.rem(d + off + n, n)))

    offs = (2, -2, 4, -4)
    mate_copy = remote(st.at[reach], st.at[reach - 1 + 2 * core], s_send.at[4],
                       s_recv.at[reach - 1 + 2 * core], (band, mate))
    mate_copy.start()
    for i, off in enumerate(offs):
        @pl.when((d + off >= 0) & (d + off < n))
        def _(i=i, off=off):
            state_to(i, off).start()

    stage_one(2)
    stage_two(0)
    stage_two(1)
    local[11].wait()
    local[12].wait()
    stage_three(0)
    stage_three(1)

    def project(e):
        def step(h, _):
            cs = pl.ds(pl.multiple_of(h * cols, cols), cols)
            rs = pl.ds(pl.multiple_of(e * rows, rows), rows)
            x = st[e]
            kp[rs, cs] = dot(x, wq[h, 1]).astype(BF)
            vp[rs, cs] = dot(x, wq[h, 2]).astype(BF)
            return 0

        lax.fori_loop(0, nh, step, 0)

    def in_range(e):
        return (d - reach + e >= 0) & (d - reach + e < n)

    def wait_slot(e):
        @pl.when(in_range(e))
        def _():
            remote(st.at[reach], st.at[e], s_send.at[4], s_recv.at[e], (band, mate)).wait_recv()

    def pass_on(i, e):
        to = e - 1 + 2 * core
        return remote(st.at[e], st.at[to], f_send.at[i], s_recv.at[to], (band, mate))

    def passes(e):
        ok = in_range(e)
        if e == 0:
            ok = ok & (core == 1)
        if e == slots - 1:
            ok = ok & (core == 0)
        return ok

    def receive(i, e):
        wait_slot(e)

        @pl.when(passes(e))
        def _():
            pass_on(i, e).start()

    project(reach)
    stage_one(3)
    wait_slot(mate_slot)
    project(mate_slot)
    stage_two(2)
    receive(0, 2)
    receive(1, 6)
    project(2)
    stage_three(2)

    def query_step(h, _):
        cs = pl.ds(pl.multiple_of(h * cols, cols), cols)
        qs[:, cs] = (dot(st[reach], wq[h, 0]).astype(BF) * scale).astype(BF)
        return 0

    lax.fori_loop(0, nh, query_step, 0)
    receive(2, 0)
    receive(3, 8)
    project(6)
    project(0)
    project(8)
    far_slot = reach - 1 + 2 * core
    for e in (far_slot, 1, 7):
        wait_slot(e)
        project(e)
    stage_two(3)

    def window_step(j, _):
        cs = pl.ds(pl.multiple_of(j * wide, wide), wide)
        q2 = pair_rows(qs[:, cs], head_size)
        scores = dot_t(q2, kp[:, cs])
        b = bias[...]
        w = softmax_rows(scores + jnp.concatenate([b, b], axis=0))
        att[:, cs] = pair_merge(dot(w, vp[:, cs]), rows, head_size).astype(BF)
        return 0

    lax.fori_loop(0, pairs, window_step, 0)
    stage_three(3)
    out[...] = (st[reach].astype(F32) + dot(att[...], wo[...])).astype(BF)

    @pl.when(jnp.logical_not(last))
    def _():
        up.wait_send()

    @pl.when(jnp.logical_not(first))
    def _():
        down.wait_send()

    for p in range(4):
        to_mate(p).wait_send()
        for k in range(1, xs):
            cross(p, k).wait_send()
            to_twin(p, k).wait_send()
            near_mate(p, k).wait_send()
            far_mate(p, k).wait_send()
    mate_copy.wait_send()
    for i, off in enumerate(offs):
        @pl.when((d + off >= 0) & (d + off < n))
        def _(i=i, off=off):
            state_to(i, off).wait_send()

    for i, e in enumerate((2, 6, 0, 8)):
        @pl.when(passes(e))
        def _(i=i, e=e):
            pass_on(i, e).wait_send()


def local(nb, nh, grid_feat, mesh_feat, enc_query, enc_keyval, enc_out, proc_qkv, proc_out,
          tile_ids, key_counts):
    rows, dm = mesh_feat.shape
    grows = grid_feat.shape[0]
    tiles = grows // GT + 2 * HALO_TILES
    slots = 2 * (HALFW // rows) + 1
    cols = proc_qkv.shape[2]
    xs = nh // 2
    dma = pltpu.SemaphoreType.DMA
    any_spec = pl.BlockSpec(memory_space=pl.ANY)
    smem = pl.BlockSpec(memory_space=pltpu.SMEM)
    pieces = (4, max(xs - 1, 1))
    return pl.pallas_call(
        functools.partial(kernel, nb, nh),
        out_shape=jax.ShapeDtypeStruct((rows, dm), BF),
        in_specs=[smem, smem] + [any_spec] * 7,
        out_specs=pl.BlockSpec(memory_space=pltpu.VMEM),
        scratch_shapes=[
            pltpu.VMEM((grows, dm), BF),
            pltpu.VMEM((2, HALO_TILES * GT, dm), BF),
            pltpu.VMEM(enc_keyval.shape, BF),
            pltpu.VMEM(enc_query.shape, BF),
            pltpu.VMEM(enc_out.shape, BF),
            pltpu.VMEM((rows, dm), BF),
            pltpu.VMEM((tiles, GT, 2 * dm), BF),
            pltpu.VMEM((nh, 3, dm, cols), BF),
            pltpu.VMEM((nh * cols, dm), BF),
            pltpu.VMEM((slots, rows, dm), BF),
            pltpu.VMEM((rows, dm), BF),
            pltpu.VMEM((rows, dm), BF),
            pltpu.VMEM((slots * rows, dm), BF),
            pltpu.VMEM((slots * rows, dm), BF),
            pltpu.VMEM((rows, slots * rows), F32),
            dma((13,)), dma((2,)), dma((2,)),
            dma((4,)), dma((4,)),
            dma(pieces), dma(pieces), dma(pieces), dma(pieces),
            dma(pieces), dma(pieces), dma(pieces), dma(pieces),
            dma((5,)), dma((slots,)), dma((4,)),
        ],
        compiler_params=pltpu.CompilerParams(
            collective_id=0, has_side_effects=True, vmem_limit_bytes=63 * 1024 * 1024),
    )(tile_ids, key_counts, grid_feat, mesh_feat, enc_query, enc_keyval, enc_out, proc_qkv,
      proc_out)


def solution(mesh):
    return jax.shard_map(
        functools.partial(local, mesh.shape["band"], mesh.shape["head"]),
        mesh=mesh,
        in_specs=(
            P(("band", "head"), None),
            P(("band", "head"), None),
            P(),
            P(),
            P(),
            P(None, None, "head"),
            P("head", None),
            P(("band", "head"), None),
            P(("band", "head")),
        ),
        out_specs=P(("band", "head"), None),
        check_vma=False,
    )
```

```python
import functools

import jax
import jax.numpy as jnp
from jax import lax
from jax.experimental import pallas as pl
from jax.experimental.pallas import tpu as pltpu
from jax.sharding import PartitionSpec as P

HEADS = 16
HALFW = 512
GT = 128
MT = 64
HALO_TILES = 2
BF = jnp.bfloat16
F32 = jnp.float32
MESH_ID = pl.DeviceIdType.MESH
NEG = -1e30
GROUP = 4


def dot(a, b):
    return jnp.dot(a, b, preferred_element_type=F32)


def dot_t(a, b):
    return lax.dot_general(a, b, (((1,), (1,)), ((), ())), preferred_element_type=F32)


def group_rows(q, count, width):
    lane = lax.broadcasted_iota(jnp.int32, q.shape, 1)
    zero = jnp.zeros_like(q)
    return jnp.concatenate(
        [jnp.where((lane >= i * width) & (lane < (i + 1) * width), q, zero)
         for i in range(count)], axis=0)


def group_merge(o, rows, count, width):
    lane = lax.broadcasted_iota(jnp.int32, (rows, count * width), 1)
    r = o[:rows]
    for i in range(1, count):
        r = jnp.where(lane < i * width, r, o[i * rows:(i + 1) * rows])
    return r


def softmax_rows(scores):
    top = jnp.max(scores, axis=-1, keepdims=True)
    weights = jnp.exp(scores - top)
    return (weights * (1.0 / jnp.sum(weights, axis=-1, keepdims=True))).astype(BF)


def kernel(
    nb, nh, tid, cnt, grid, feat_h, wquery_h, wkv_h, wenc_h, qkv_h, pout_h, out,
    g, halo, wkv, wquery, wenc, feat, kv, wq, wo, st, qs, att, qh, kp, vp, mine, got, bias,
    lsem, hs_send, hs_recv, w_send, w_recv, ox_send, ox_recv, op_send, op_recv,
    m_send, x_send, v_send, r_send, p_send, s_recv, a_send, a_recv,
):
    n = nb * nh
    band = lax.axis_index("band")
    head = lax.axis_index("head")
    d = band * nh + head
    core = lax.rem(head, 2)
    x = head // 2
    mate = head + 1 - 2 * core
    xs = nh // 2
    rows, dm = feat.shape
    tiles = grid.shape[0] // GT
    edge = HALO_TILES * GT
    cols = qkv_h.shape[2]
    slots = st.shape[0]
    reach = HALFW // rows
    hop = reach // 2
    halves = rows // MT
    head_size = dm // HEADS
    wide = GROUP * head_size
    scale = head_size ** (-0.5)

    def flat_id(f):
        return (f // nh, lax.rem(f, nh))

    def remote(src, dst, ss, rs, dev):
        return pltpu.make_async_remote_copy(
            src_ref=src, dst_ref=dst, send_sem=ss, recv_sem=rs, device_id=dev,
            device_id_type=MESH_ID)

    gchunk = g.shape[0] // 4
    wchunk = wkv.shape[1] // 4
    local = []
    for i in range(4):
        local.append(pltpu.make_async_copy(
            wkv_h.at[:, pl.ds(i * wchunk, wchunk)], wkv.at[:, pl.ds(i * wchunk, wchunk)],
            lsem.at[i]))
        local.append(pltpu.make_async_copy(
            grid.at[pl.ds(i * gchunk, gchunk)], g.at[pl.ds(i * gchunk, gchunk)], lsem.at[4 + i]))
    local.append(pltpu.make_async_copy(feat_h, feat, lsem.at[8]))
    local.append(pltpu.make_async_copy(wquery_h, wquery, lsem.at[9]))
    local.append(pltpu.make_async_copy(wenc_h, wenc, lsem.at[10]))
    local.append(pltpu.make_async_copy(qkv_h, wq.at[core], lsem.at[11]))

    def out_rows(src):
        return wo.at[pl.ds(pl.multiple_of(src * cols, cols), cols)]

    local.append(pltpu.make_async_copy(pout_h, out_rows(head), lsem.at[12]))
    for c in local:
        c.start()

    def same_core(k):
        return (band, lax.rem(head + 2 * k, nh))

    def same_core_src(h, k):
        return lax.rem(h - 2 * k + nh, nh)

    bar = pltpu.get_barrier_semaphore()
    expect = jnp.int32(0)
    for off in (-nh, -1, 1, nh):
        ok = (d + off >= 0) & (d + off < n)
        expect = expect + ok.astype(jnp.int32)

        @pl.when(ok)
        def _(off=off):
            pl.semaphore_signal(bar, inc=1, device_id=flat_id(d + off), device_id_type=MESH_ID)

    for k in range(1, xs):
        pl.semaphore_signal(bar, inc=1, device_id=same_core(k), device_id_type=MESH_ID)
    pl.semaphore_signal(bar, inc=1, device_id=(band, mate), device_id_type=MESH_ID)
    pl.semaphore_wait(bar, expect + xs)

    first, last = d == 0, d == n - 1
    up = remote(grid.at[pl.ds(grid.shape[0] - edge, edge)], halo.at[0], hs_send.at[0],
                hs_recv.at[0], flat_id(lax.rem(d + 1, n)))
    down = remote(grid.at[pl.ds(0, edge)], halo.at[1], hs_send.at[1], hs_recv.at[1],
                  flat_id(lax.rem(d + n - 1, n)))

    @pl.when(jnp.logical_not(last))
    def _():
        up.start()

    @pl.when(jnp.logical_not(first))
    def _():
        down.start()

    @pl.when(first)
    def _():
        halo[0] = jnp.zeros(halo.shape[1:], BF)

    @pl.when(last)
    def _():
        halo[1] = jnp.zeros(halo.shape[1:], BF)

    qkv_mate = remote(qkv_h, wq.at[core], w_send.at[0], w_recv.at[0], (band, mate))
    out_mate = remote(pout_h, out_rows(head), w_send.at[1], w_recv.at[1], (band, mate))

    def out_cross(k):
        return remote(pout_h, out_rows(head), ox_send.at[k - 1], ox_recv.at[k - 1], same_core(k))

    def out_pass(k):
        src = out_rows(same_core_src(head, k))
        return remote(src, src, op_send.at[k - 1], op_recv.at[k - 1], (band, mate))

    for k in range(1, xs):
        out_cross(k).start()
    qkv_mate.start()
    out_mate.start()

    below, above = band > 0, band < nb - 1
    for e in range(slots):
        if e < reach:
            ok = below
        elif e >= nh + reach:
            ok = above
        else:
            continue
        if e == 0:
            ok = ok & (core == 0)
        if e == slots - 1:
            ok = ok & (core == 1)

        @pl.when(jnp.logical_not(ok))
        def _(e=e):
            st[e] = jnp.zeros(st.shape[1:], BF)

    span = (2 * reach + 1) * rows
    brow = lax.broadcasted_iota(jnp.int32, (rows, span), 0)
    bcol = lax.broadcasted_iota(jnp.int32, (rows, span), 1)
    near = (bcol - HALFW - brow < HALFW) & (bcol - HALFW - brow > -HALFW)
    for q in range(xs):
        kpos = (band * nh + 2 * q + core - reach) * rows + bcol
        bias[q] = jnp.where(near & (kpos >= 0) & (kpos < n * rows), 0.0, NEG).astype(F32)

    for i in range(4):
        local[2 * i].wait()
    for i in range(4):
        local[2 * i + 1].wait()
        ct = gchunk // GT

        def col_step(j, _, i=i, ct=ct):
            cs = pl.ds(pl.multiple_of(j * wchunk, wchunk), wchunk)
            r = dot(g[pl.ds(i * gchunk, gchunk)], wkv[:, cs]).astype(BF)
            kv[pl.ds(HALO_TILES + i * ct, ct), :, cs] = r.reshape(ct, GT, wchunk)
            return 0

        lax.fori_loop(0, 4, col_step, 0)
    local[8].wait()
    local[9].wait()
    local[10].wait()
    qs[...] = (dot(feat[...], wquery[...]).astype(BF) * scale).astype(BF)

    @pl.when(jnp.logical_not(first))
    def _():
        up.wait_recv()

    @pl.when(jnp.logical_not(last))
    def _():
        down.wait_recv()

    def halo_step(j, _):
        cs = pl.ds(pl.multiple_of(j * wchunk, wchunk), wchunk)
        r = dot(halo[...].reshape(2 * edge, dm), wkv[:, cs]).astype(BF)
        r = r.reshape(2 * HALO_TILES, GT, wchunk)
        kv[pl.ds(0, HALO_TILES), :, cs] = r[:HALO_TILES]
        kv[pl.ds(HALO_TILES + tiles, HALO_TILES), :, cs] = r[HALO_TILES:]
        return 0

    lax.fori_loop(0, 4, halo_step, 0)

    own = head + reach
    to_above = above & (x >= xs - hop)
    to_below = below & (x < hop)

    def part(e, u):
        return st.at[e, pl.ds(u * MT, MT)]

    def state_mate(u):
        return remote(part(own, u), part(own, u), m_send.at[u], s_recv.at[own, u], (band, mate))

    def state_x(k, u):
        return remote(part(own, u), part(own, u), x_send.at[k - 1, u], s_recv.at[own, u],
                      same_core(k))

    def state_v(i, u):
        sign = 1 - 2 * i
        to = own - sign * nh
        to = jnp.clip(to, 0, slots - 1)
        dev = (jnp.clip(band + sign, 0, nb - 1), head)
        return remote(part(own, u), part(to, u), v_send.at[i, u], s_recv.at[to, u], dev)

    base = d * tiles - HALO_TILES
    lists = tid.shape[1]
    for m in range(halves):
        ids = [jnp.clip(tid[m, s] - base, 0, kv.shape[0] - 1) for s in range(lists)]
        valid = cnt[m]

        def group_step(j, _, m=m, ids=ids, valid=valid):
            cs = pl.ds(pl.multiple_of(j * wide, wide), wide)
            vs = pl.ds(pl.multiple_of(dm + j * wide, wide), wide)
            q2 = group_rows(qs[pl.ds(m * MT, MT), cs], GROUP, head_size)
            k2 = jnp.concatenate([kv[t, :, cs] for t in ids], axis=0)
            scores = dot_t(q2, k2)
            pos = lax.broadcasted_iota(jnp.int32, scores.shape, 1)
            w = softmax_rows(jnp.where(pos < valid, scores, NEG))
            v2 = jnp.concatenate([kv[t, :, vs] for t in ids], axis=0)
            att[pl.ds(m * MT, MT), cs] = group_merge(dot(w, v2), MT, GROUP, head_size).astype(BF)
            return 0

        lax.fori_loop(0, HEADS // GROUP, group_step, 0, unroll=2)
        ms = pl.ds(m * MT, MT)
        st[own, ms] = (feat[ms].astype(F32) + dot(att[ms], wenc[...])).astype(BF)
        for k in range(1, xs):
            state_x(k, m).start()
        for i, ok in enumerate((to_above, to_below)):
            @pl.when(ok)
            def _(i=i, m=m):
                state_v(i, m).start()
        state_mate(m).start()

    def arrived(e, u):
        remote(part(own, u), part(e, u), m_send.at[u], s_recv.at[e, u], (band, mate)).wait_recv()

    def slot_of(j):
        return 2 * j + core

    def mate_slot(j):
        return 2 * j + 1 - core

    def hand(j, u):
        e = slot_of(j)
        return remote(part(e, u), part(e, u), p_send.at[j, u], s_recv.at[e, u], (band, mate))

    def wanted(j):
        e = slot_of(j)
        return (e >= 1 - core) & (e <= slots - 1 - core)

    def relay(i, k, j, u):
        e = slot_of(j)
        return remote(part(e, u), part(e, u), r_send.at[i, k - 1, u], s_recv.at[e, u],
                      same_core(k))

    def project(j):
        def step(h, _):
            cs = pl.ds(pl.multiple_of(h * cols, cols), cols)
            rs = pl.ds(pl.multiple_of(j * 2 * rows, 2 * rows), 2 * rows)
            y = st[pl.ds(2 * j, 2)].reshape(2 * rows, dm)
            kp[rs, cs] = dot(y, wq[h, 1]).astype(BF)
            vp[rs, cs] = dot(y, wq[h, 2]).astype(BF)
            return 0

        lax.fori_loop(0, 2, step, 0)

    def from_mate(j):
        e = mate_slot(j)
        ok = (e >= core) & (e <= slots - 2 + core)
        if isinstance(j, int):
            if j < hop:
                ok = ok & below
            elif j >= xs + hop:
                ok = ok & above
        else:
            ok = ok & ((j >= hop) | below) & ((j < xs + hop) | above)

        @pl.when(ok)
        def _():
            for u in range(halves):
                arrived(e, u)

    def query(q):
        def step(h, _):
            cs = pl.ds(pl.multiple_of(h * cols, cols), cols)
            y = st[slot_of(q + hop)]
            qh[q, :, cs] = (dot(y, wq[h, 0]).astype(BF) * scale).astype(BF)
            return 0

        lax.fori_loop(0, 2, step, 0)

    local[11].wait()
    local[12].wait()
    remote(qkv_h, wq.at[1 - core], w_send.at[0], w_recv.at[0], (band, mate)).wait_recv()
    from_mate(x + hop)
    project(x + hop)

    others = [lax.rem(x + k, xs) for k in range(1, xs)]
    for q in others:
        for u in range(halves):
            arrived(slot_of(q + hop), u)
            hand(q + hop, u).start()

    direct = ((x + hop - xs, below & (x >= xs - hop)), (x + hop + xs, above & (x < hop)))

    def take_direct(u):
        for i, (j, ok) in enumerate(direct):
            @pl.when(ok)
            def _(i=i, j=j):
                arrived(slot_of(j), u)
                for k in range(1, xs):
                    relay(i, k, j, u).start()

            @pl.when(ok & wanted(j))
            def _(j=j):
                hand(j, u).start()

    take_direct(0)
    query(x)
    for u in range(1, halves):
        take_direct(u)
    for k in range(1, xs):
        src = out_rows(same_core_src(head, k))
        remote(pout_h, src, ox_send.at[k - 1], ox_recv.at[k - 1], same_core(k)).wait_recv()
        out_pass(k).start()
    for q in others:
        from_mate(q + hop)
        project(q + hop)
        query(q)

    far = []
    for j in range(hop):
        far.append((j, below & (x != xs - hop + j)))
    for j in range(hop):
        far.append((xs + hop + j, above & (x != j)))
    for u in range(halves):
        for j, ok in far:
            @pl.when(ok)
            def _(j=j, u=u):
                arrived(slot_of(j), u)

            @pl.when(ok & wanted(j))
            def _(j=j, u=u):
                hand(j, u).start()
    for j, _ in far:
        from_mate(j)
        project(j)

    half_cols = qh.shape[2]

    def att_to(k):
        return remote(mine.at[k], got.at[x], a_send.at[k - 1], a_recv.at[k - 1], same_core(k))

    def window(q, dst):
        rs = pl.ds(pl.multiple_of((2 * q + core) * rows, rows), span)

        def step(j, _):
            cs = pl.ds(pl.multiple_of(j * wide, wide), wide)
            q2 = group_rows(qh[q, :, cs], GROUP, head_size)
            b = bias[q]
            scores = dot_t(q2, kp[rs, cs]) + jnp.concatenate([b] * GROUP, axis=0)
            o = dot(softmax_rows(scores), vp[rs, cs])
            mine[dst, :, cs] = group_merge(o, rows, GROUP, head_size).astype(BF)
            return 0

        steps = half_cols // wide
        lax.fori_loop(0, steps, step, 0, unroll=min(steps, 2))

    for k in range(1, xs):
        window(lax.rem(x + k, xs), k)
        att_to(k).start()
    window(x, 0)

    def out_block(q):
        return wo[pl.ds(pl.multiple_of(q * half_cols, half_cols), half_cols)]

    remote(pout_h, out_rows(mate), w_send.at[1], w_recv.at[1], (band, mate)).wait_recv()
    for k in range(1, xs):
        src = out_rows(same_core_src(mate, k))
        remote(pout_h, src, op_send.at[k - 1], op_recv.at[k - 1], (band, mate)).wait_recv()
    total = st[own].astype(F32) + dot(mine[0], out_block(x))
    for k in range(1, xs):
        src = lax.rem(x - k + xs, xs)
        remote(mine.at[k], got.at[src], a_send.at[k - 1], a_recv.at[k - 1],
               same_core(k)).wait_recv()
        total = total + dot(got[src], out_block(src))
    out[...] = total.astype(BF)

    @pl.when(jnp.logical_not(last))
    def _():
        up.wait_send()

    @pl.when(jnp.logical_not(first))
    def _():
        down.wait_send()

    qkv_mate.wait_send()
    out_mate.wait_send()
    for k in range(1, xs):
        out_cross(k).wait_send()
        out_pass(k).wait_send()
        att_to(k).wait_send()
    for u in range(halves):
        state_mate(u).wait_send()
        for k in range(1, xs):
            state_x(k, u).wait_send()
        for i, ok in enumerate((to_above, to_below)):
            @pl.when(ok)
            def _(i=i, u=u):
                state_v(i, u).wait_send()
        for q in others:
            hand(q + hop, u).wait_send()
        for i, (j, ok) in enumerate(direct):
            @pl.when(ok)
            def _(i=i, j=j, u=u):
                for k in range(1, xs):
                    relay(i, k, j, u).wait_send()

            @pl.when(ok & wanted(j))
            def _(j=j, u=u):
                hand(j, u).wait_send()
        for j, ok in far:
            @pl.when(ok & wanted(j))
            def _(j=j, u=u):
                hand(j, u).wait_send()


def local(nb, nh, grid_feat, mesh_feat, enc_query, enc_keyval, enc_out, proc_qkv, proc_out,
          tile_ids, key_counts):
    rows, dm = mesh_feat.shape
    grows = grid_feat.shape[0]
    tiles = grows // GT + 2 * HALO_TILES
    reach = HALFW // rows
    slots = nh + 2 * reach
    cols = proc_qkv.shape[2]
    xs = nh // 2
    nx = max(xs - 1, 1)
    halves = rows // MT
    dma = pltpu.SemaphoreType.DMA
    any_spec = pl.BlockSpec(memory_space=pl.ANY)
    smem = pl.BlockSpec(memory_space=pltpu.SMEM)
    return pl.pallas_call(
        functools.partial(kernel, nb, nh),
        out_shape=jax.ShapeDtypeStruct((rows, dm), BF),
        in_specs=[smem, smem] + [any_spec] * 7,
        out_specs=pl.BlockSpec(memory_space=pltpu.VMEM),
        scratch_shapes=[
            pltpu.VMEM((grows, dm), BF),
            pltpu.VMEM((2, HALO_TILES * GT, dm), BF),
            pltpu.VMEM(enc_keyval.shape, BF),
            pltpu.VMEM(enc_query.shape, BF),
            pltpu.VMEM(enc_out.shape, BF),
            pltpu.VMEM((rows, dm), BF),
            pltpu.VMEM((tiles, GT, 2 * dm), BF),
            pltpu.VMEM((2, 3, dm, cols), BF),
            pltpu.VMEM((nh * cols, dm), BF),
            pltpu.VMEM((slots, rows, dm), BF),
            pltpu.VMEM((rows, dm), BF),
            pltpu.VMEM((rows, dm), BF),
            pltpu.VMEM((xs, rows, 2 * cols), BF),
            pltpu.VMEM((slots * rows, 2 * cols), BF),
            pltpu.VMEM((slots * rows, 2 * cols), BF),
            pltpu.VMEM((xs, rows, 2 * cols), BF),
            pltpu.VMEM((xs, rows, 2 * cols), BF),
            pltpu.VMEM((xs, rows, (2 * reach + 1) * rows), F32),
            dma((13,)), dma((2,)), dma((2,)), dma((2,)), dma((2,)),
            dma((nx,)), dma((nx,)), dma((nx,)), dma((nx,)),
            dma((halves,)), dma((nx, halves)), dma((2, halves)), dma((2, nx, halves)),
            dma((slots // 2, halves)), dma((slots, halves)), dma((nx,)), dma((nx,)),
        ],
        compiler_params=pltpu.CompilerParams(
            collective_id=0, has_side_effects=True, vmem_limit_bytes=63 * 1024 * 1024),
    )(tile_ids, key_counts, grid_feat, mesh_feat, enc_query, enc_keyval, enc_out, proc_qkv,
      proc_out)


def solution(mesh):
    return jax.shard_map(
        functools.partial(local, mesh.shape["band"], mesh.shape["head"]),
        mesh=mesh,
        in_specs=(
            P(("band", "head"), None),
            P(("band", "head"), None),
            P(),
            P(),
            P(),
            P(None, None, "head"),
            P("head", None),
            P(("band", "head"), None),
            P(("band", "head")),
        ),
        out_specs=P(("band", "head"), None),
        check_vma=False,
    )
```

```python
import functools

import jax
import jax.numpy as jnp
from jax import lax
from jax.experimental import pallas as pl
from jax.experimental.pallas import tpu as pltpu
from jax.sharding import PartitionSpec as P

HEADS = 16
HALFW = 512
GT = 128
MT = 64
HALO_TILES = 2
BF = jnp.bfloat16
F32 = jnp.float32
MESH_ID = pl.DeviceIdType.MESH
NEG = -1e30
GROUP = 4


def dot(a, b):
    return jnp.dot(a, b, preferred_element_type=F32)


def dot_t(a, b):
    return lax.dot_general(a, b, (((1,), (1,)), ((), ())), preferred_element_type=F32)


def group_rows(q, count, width):
    lane = lax.broadcasted_iota(jnp.int32, q.shape, 1)
    zero = jnp.zeros_like(q)
    return jnp.concatenate(
        [jnp.where((lane >= i * width) & (lane < (i + 1) * width), q, zero)
         for i in range(count)], axis=0)


def group_merge(o, rows, count, width):
    lane = lax.broadcasted_iota(jnp.int32, (rows, count * width), 1)
    r = o[:rows]
    for i in range(1, count):
        r = jnp.where(lane < i * width, r, o[i * rows:(i + 1) * rows])
    return r


def softmax_rows(scores):
    top = jnp.max(scores, axis=-1, keepdims=True)
    weights = jnp.exp(scores - top)
    return (weights * (1.0 / jnp.sum(weights, axis=-1, keepdims=True))).astype(BF)


def kernel(
    nb, nh, tid, cnt, grid, feat_h, wquery_h, wkv_h, wenc_h, qkv_h, pout_h, out,
    g, halo, wkv, wquery, wenc, feat, kv, wq, wo, st, qs, att, qh, kp, vp, mine, got, bias,
    lsem, hs_send, hs_recv, w_send, w_recv, ox_send, ox_recv, op_send, op_recv,
    m_send, x_send, v_send, r_send, p_send, s_recv, a_send, a_recv,
):
    n = nb * nh
    band = lax.axis_index("band")
    head = lax.axis_index("head")
    d = band * nh + head
    core = lax.rem(head, 2)
    x = head // 2
    mate = head + 1 - 2 * core
    xs = nh // 2
    rows, dm = feat.shape
    tiles = grid.shape[0] // GT
    edge = HALO_TILES * GT
    cols = qkv_h.shape[2]
    slots = st.shape[0]
    reach = HALFW // rows
    hop = reach // 2
    halves = rows // MT
    head_size = dm // HEADS
    wide = GROUP * head_size
    scale = head_size ** (-0.5)

    def flat_id(f):
        return (f // nh, lax.rem(f, nh))

    def remote(src, dst, ss, rs, dev):
        return pltpu.make_async_remote_copy(
            src_ref=src, dst_ref=dst, send_sem=ss, recv_sem=rs, device_id=dev,
            device_id_type=MESH_ID)

    gchunk = g.shape[0] // 4
    wchunk = wkv.shape[1] // 4
    local = []
    for i in range(4):
        local.append(pltpu.make_async_copy(
            wkv_h.at[:, pl.ds(i * wchunk, wchunk)], wkv.at[:, pl.ds(i * wchunk, wchunk)],
            lsem.at[i]))
        local.append(pltpu.make_async_copy(
            grid.at[pl.ds(i * gchunk, gchunk)], g.at[pl.ds(i * gchunk, gchunk)], lsem.at[4 + i]))
    local.append(pltpu.make_async_copy(feat_h, feat, lsem.at[8]))
    local.append(pltpu.make_async_copy(wquery_h, wquery, lsem.at[9]))
    local.append(pltpu.make_async_copy(wenc_h, wenc, lsem.at[10]))
    local.append(pltpu.make_async_copy(qkv_h, wq.at[core], lsem.at[11]))

    def out_rows(src):
        return wo.at[pl.ds(pl.multiple_of(src * cols, cols), cols)]

    local.append(pltpu.make_async_copy(pout_h, out_rows(head), lsem.at[12]))
    for c in local:
        c.start()

    def same_core(k):
        return (band, lax.rem(head + 2 * k, nh))

    def same_core_src(h, k):
        return lax.rem(h - 2 * k + nh, nh)

    bar = pltpu.get_barrier_semaphore()
    expect = jnp.int32(0)
    for off in (-nh, -1, 1, nh):
        ok = (d + off >= 0) & (d + off < n)
        expect = expect + ok.astype(jnp.int32)

        @pl.when(ok)
        def _(off=off):
            pl.semaphore_signal(bar, inc=1, device_id=flat_id(d + off), device_id_type=MESH_ID)

    for k in range(1, xs):
        pl.semaphore_signal(bar, inc=1, device_id=same_core(k), device_id_type=MESH_ID)
    pl.semaphore_signal(bar, inc=1, device_id=(band, mate), device_id_type=MESH_ID)
    pl.semaphore_wait(bar, expect + xs)

    first, last = d == 0, d == n - 1
    up = remote(grid.at[pl.ds(grid.shape[0] - edge, edge)], halo.at[0], hs_send.at[0],
                hs_recv.at[0], flat_id(lax.rem(d + 1, n)))
    down = remote(grid.at[pl.ds(0, edge)], halo.at[1], hs_send.at[1], hs_recv.at[1],
                  flat_id(lax.rem(d + n - 1, n)))

    @pl.when(jnp.logical_not(last))
    def _():
        up.start()

    @pl.when(jnp.logical_not(first))
    def _():
        down.start()

    @pl.when(first)
    def _():
        halo[0] = jnp.zeros(halo.shape[1:], BF)

    @pl.when(last)
    def _():
        halo[1] = jnp.zeros(halo.shape[1:], BF)

    qkv_mate = remote(qkv_h, wq.at[core], w_send.at[0], w_recv.at[0], (band, mate))
    out_mate = remote(pout_h, out_rows(head), w_send.at[1], w_recv.at[1], (band, mate))

    def out_cross(k):
        return remote(pout_h, out_rows(head), ox_send.at[k - 1], ox_recv.at[k - 1], same_core(k))

    def out_pass(k):
        src = out_rows(same_core_src(head, k))
        return remote(src, src, op_send.at[k - 1], op_recv.at[k - 1], (band, mate))

    qkv_mate.start()
    out_mate.start()

    below, above = band > 0, band < nb - 1
    for e in range(slots):
        if e < reach:
            ok = below
        elif e >= nh + reach:
            ok = above
        else:
            continue
        if e == 0:
            ok = ok & (core == 0)
        if e == slots - 1:
            ok = ok & (core == 1)

        @pl.when(jnp.logical_not(ok))
        def _(e=e):
            st[e] = jnp.zeros(st.shape[1:], BF)

    span = (2 * reach + 1) * rows
    brow = lax.broadcasted_iota(jnp.int32, (rows, span), 0)
    bcol = lax.broadcasted_iota(jnp.int32, (rows, span), 1)
    near = (bcol - HALFW - brow < HALFW) & (bcol - HALFW - brow > -HALFW)
    for q in range(xs):
        kpos = (band * nh + 2 * q + core - reach) * rows + bcol
        bias[q] = jnp.where(near & (kpos >= 0) & (kpos < n * rows), 0.0, NEG).astype(F32)

    for i in range(4):
        local[2 * i].wait()
    for i in range(4):
        local[2 * i + 1].wait()
        ct = gchunk // GT

        def col_step(j, _, i=i, ct=ct):
            cs = pl.ds(pl.multiple_of(j * wchunk, wchunk), wchunk)
            r = dot(g[pl.ds(i * gchunk, gchunk)], wkv[:, cs]).astype(BF)
            kv[pl.ds(HALO_TILES + i * ct, ct), :, cs] = r.reshape(ct, GT, wchunk)
            return 0

        lax.fori_loop(0, 4, col_step, 0)
    local[8].wait()
    local[9].wait()
    local[10].wait()
    qs[...] = (dot(feat[...], wquery[...]).astype(BF) * scale).astype(BF)

    @pl.when(jnp.logical_not(first))
    def _():
        up.wait_recv()

    @pl.when(jnp.logical_not(last))
    def _():
        down.wait_recv()

    def halo_step(j, _):
        cs = pl.ds(pl.multiple_of(j * wchunk, wchunk), wchunk)
        r = dot(halo[...].reshape(2 * edge, dm), wkv[:, cs]).astype(BF)
        r = r.reshape(2 * HALO_TILES, GT, wchunk)
        kv[pl.ds(0, HALO_TILES), :, cs] = r[:HALO_TILES]
        kv[pl.ds(HALO_TILES + tiles, HALO_TILES), :, cs] = r[HALO_TILES:]
        return 0

    lax.fori_loop(0, 4, halo_step, 0)

    own = head + reach
    to_above = above & (x >= xs - hop)
    to_below = below & (x < hop)

    def part(e, u):
        return st.at[e, pl.ds(u * MT, MT)]

    def state_mate(u):
        return remote(part(own, u), part(own, u), m_send.at[u], s_recv.at[own, u], (band, mate))

    def state_x(k, u):
        return remote(part(own, u), part(own, u), x_send.at[k - 1, u], s_recv.at[own, u],
                      same_core(k))

    def state_v(i, u):
        sign = 1 - 2 * i
        to = own - sign * nh
        to = jnp.clip(to, 0, slots - 1)
        dev = (jnp.clip(band + sign, 0, nb - 1), head)
        return remote(part(own, u), part(to, u), v_send.at[i, u], s_recv.at[to, u], dev)

    base = d * tiles - HALO_TILES
    lists = tid.shape[1]
    for m in range(halves):
        ids = [jnp.clip(tid[m, s] - base, 0, kv.shape[0] - 1) for s in range(lists)]
        valid = cnt[m]

        def group_step(j, _, m=m, ids=ids, valid=valid):
            cs = pl.ds(pl.multiple_of(j * wide, wide), wide)
            vs = pl.ds(pl.multiple_of(dm + j * wide, wide), wide)
            q2 = group_rows(qs[pl.ds(m * MT, MT), cs], GROUP, head_size)
            k2 = jnp.concatenate([kv[t, :, cs] for t in ids], axis=0)
            scores = dot_t(q2, k2)
            pos = lax.broadcasted_iota(jnp.int32, scores.shape, 1)
            w = softmax_rows(jnp.where(pos < valid, scores, NEG))
            v2 = jnp.concatenate([kv[t, :, vs] for t in ids], axis=0)
            att[pl.ds(m * MT, MT), cs] = group_merge(dot(w, v2), MT, GROUP, head_size).astype(BF)
            return 0

        lax.fori_loop(0, HEADS // GROUP, group_step, 0, unroll=2)
        ms = pl.ds(m * MT, MT)
        st[own, ms] = (feat[ms].astype(F32) + dot(att[ms], wenc[...])).astype(BF)
        for k in range(1, xs):
            state_x(k, m).start()
        for i, ok in enumerate((to_above, to_below)):
            @pl.when(ok)
            def _(i=i, m=m):
                state_v(i, m).start()
        state_mate(m).start()

    def arrived(e, u):
        remote(part(own, u), part(e, u), m_send.at[u], s_recv.at[e, u], (band, mate)).wait_recv()

    def slot_of(j):
        return 2 * j + core

    def mate_slot(j):
        return 2 * j + 1 - core

    def hand(j, u):
        e = slot_of(j)
        return remote(part(e, u), part(e, u), p_send.at[j, u], s_recv.at[e, u], (band, mate))

    def wanted(j):
        e = slot_of(j)
        return (e >= 1 - core) & (e <= slots - 1 - core)

    def relay(i, k, j, u):
        e = slot_of(j)
        return remote(part(e, u), part(e, u), r_send.at[i, k - 1, u], s_recv.at[e, u],
                      same_core(k))

    def project(j):
        def step(h, _):
            cs = pl.ds(pl.multiple_of(h * cols, cols), cols)
            rs = pl.ds(pl.multiple_of(j * 2 * rows, 2 * rows), 2 * rows)
            y = st[pl.ds(2 * j, 2)].reshape(2 * rows, dm)
            kp[rs, cs] = dot(y, wq[h, 1]).astype(BF)
            vp[rs, cs] = dot(y, wq[h, 2]).astype(BF)
            return 0

        lax.fori_loop(0, 2, step, 0)

    def from_mate(j):
        e = mate_slot(j)
        ok = (e >= core) & (e <= slots - 2 + core)
        if isinstance(j, int):
            if j < hop:
                ok = ok & below
            elif j >= xs + hop:
                ok = ok & above
        else:
            ok = ok & ((j >= hop) | below) & ((j < xs + hop) | above)

        @pl.when(ok)
        def _():
            for u in range(halves):
                arrived(e, u)

    def query(q):
        def step(h, _):
            cs = pl.ds(pl.multiple_of(h * cols, cols), cols)
            y = st[slot_of(q + hop)]
            qh[q, :, cs] = (dot(y, wq[h, 0]).astype(BF) * scale).astype(BF)
            return 0

        lax.fori_loop(0, 2, step, 0)

    local[11].wait()
    local[12].wait()
    remote(qkv_h, wq.at[1 - core], w_send.at[0], w_recv.at[0], (band, mate)).wait_recv()
    from_mate(x + hop)
    project(x + hop)

    others = [lax.rem(x + k, xs) for k in range(1, xs)]
    for q in others:
        for u in range(halves):
            arrived(slot_of(q + hop), u)
            hand(q + hop, u).start()

    direct = ((x + hop - xs, below & (x >= xs - hop)), (x + hop + xs, above & (x < hop)))

    def take_direct(u):
        for i, (j, ok) in enumerate(direct):
            @pl.when(ok)
            def _(i=i, j=j):
                arrived(slot_of(j), u)
                for k in range(1, xs):
                    relay(i, k, j, u).start()

            @pl.when(ok & wanted(j))
            def _(j=j):
                hand(j, u).start()

    take_direct(0)
    query(x)
    for u in range(1, halves):
        take_direct(u)
    for k in range(1, xs):
        out_cross(k).start()
    for q in others:
        from_mate(q + hop)
        project(q + hop)
        query(q)

    far = []
    for j in range(hop):
        far.append((j, below & (x != xs - hop + j)))
    for j in range(hop):
        far.append((xs + hop + j, above & (x != j)))
    for u in range(halves):
        for j, ok in far:
            @pl.when(ok)
            def _(j=j, u=u):
                arrived(slot_of(j), u)

            @pl.when(ok & wanted(j))
            def _(j=j, u=u):
                hand(j, u).start()
    for j, _ in far:
        from_mate(j)
        project(j)

    half_cols = qh.shape[2]

    def att_to(k):
        return remote(mine.at[k], got.at[x], a_send.at[k - 1], a_recv.at[k - 1], same_core(k))

    def window(q, dst):
        rs = pl.ds(pl.multiple_of((2 * q + core) * rows, rows), span)

        def step(j, _):
            cs = pl.ds(pl.multiple_of(j * wide, wide), wide)
            q2 = group_rows(qh[q, :, cs], GROUP, head_size)
            b = bias[q]
            scores = dot_t(q2, kp[rs, cs]) + jnp.concatenate([b] * GROUP, axis=0)
            o = dot(softmax_rows(scores), vp[rs, cs])
            mine[dst, :, cs] = group_merge(o, rows, GROUP, head_size).astype(BF)
            return 0

        steps = half_cols // wide
        lax.fori_loop(0, steps, step, 0, unroll=min(steps, 2))

    for k in range(1, xs):
        window(lax.rem(x + k, xs), k)
        att_to(k).start()
    for k in range(1, xs):
        src = out_rows(same_core_src(head, k))
        remote(pout_h, src, ox_send.at[k - 1], ox_recv.at[k - 1], same_core(k)).wait_recv()
        out_pass(k).start()
    window(x, 0)

    def out_block(q):
        return wo[pl.ds(pl.multiple_of(q * half_cols, half_cols), half_cols)]

    remote(pout_h, out_rows(mate), w_send.at[1], w_recv.at[1], (band, mate)).wait_recv()
    for k in range(1, xs):
        src = out_rows(same_core_src(mate, k))
        remote(pout_h, src, op_send.at[k - 1], op_recv.at[k - 1], (band, mate)).wait_recv()
    total = st[own].astype(F32) + dot(mine[0], out_block(x))
    for k in range(1, xs):
        src = lax.rem(x - k + xs, xs)
        remote(mine.at[k], got.at[src], a_send.at[k - 1], a_recv.at[k - 1],
               same_core(k)).wait_recv()
        total = total + dot(got[src], out_block(src))
    out[...] = total.astype(BF)

    @pl.when(jnp.logical_not(last))
    def _():
        up.wait_send()

    @pl.when(jnp.logical_not(first))
    def _():
        down.wait_send()

    qkv_mate.wait_send()
    out_mate.wait_send()
    for k in range(1, xs):
        out_cross(k).wait_send()
        out_pass(k).wait_send()
        att_to(k).wait_send()
    for u in range(halves):
        state_mate(u).wait_send()
        for k in range(1, xs):
            state_x(k, u).wait_send()
        for i, ok in enumerate((to_above, to_below)):
            @pl.when(ok)
            def _(i=i, u=u):
                state_v(i, u).wait_send()
        for q in others:
            hand(q + hop, u).wait_send()
        for i, (j, ok) in enumerate(direct):
            @pl.when(ok)
            def _(i=i, j=j, u=u):
                for k in range(1, xs):
                    relay(i, k, j, u).wait_send()

            @pl.when(ok & wanted(j))
            def _(j=j, u=u):
                hand(j, u).wait_send()
        for j, ok in far:
            @pl.when(ok & wanted(j))
            def _(j=j, u=u):
                hand(j, u).wait_send()


def local(nb, nh, grid_feat, mesh_feat, enc_query, enc_keyval, enc_out, proc_qkv, proc_out,
          tile_ids, key_counts):
    rows, dm = mesh_feat.shape
    grows = grid_feat.shape[0]
    tiles = grows // GT + 2 * HALO_TILES
    reach = HALFW // rows
    slots = nh + 2 * reach
    cols = proc_qkv.shape[2]
    xs = nh // 2
    nx = max(xs - 1, 1)
    halves = rows // MT
    dma = pltpu.SemaphoreType.DMA
    any_spec = pl.BlockSpec(memory_space=pl.ANY)
    smem = pl.BlockSpec(memory_space=pltpu.SMEM)
    return pl.pallas_call(
        functools.partial(kernel, nb, nh),
        out_shape=jax.ShapeDtypeStruct((rows, dm), BF),
        in_specs=[smem, smem] + [any_spec] * 7,
        out_specs=pl.BlockSpec(memory_space=pltpu.VMEM),
        scratch_shapes=[
            pltpu.VMEM((grows, dm), BF),
            pltpu.VMEM((2, HALO_TILES * GT, dm), BF),
            pltpu.VMEM(enc_keyval.shape, BF),
            pltpu.VMEM(enc_query.shape, BF),
            pltpu.VMEM(enc_out.shape, BF),
            pltpu.VMEM((rows, dm), BF),
            pltpu.VMEM((tiles, GT, 2 * dm), BF),
            pltpu.VMEM((2, 3, dm, cols), BF),
            pltpu.VMEM((nh * cols, dm), BF),
            pltpu.VMEM((slots, rows, dm), BF),
            pltpu.VMEM((rows, dm), BF),
            pltpu.VMEM((rows, dm), BF),
            pltpu.VMEM((xs, rows, 2 * cols), BF),
            pltpu.VMEM((slots * rows, 2 * cols), BF),
            pltpu.VMEM((slots * rows, 2 * cols), BF),
            pltpu.VMEM((xs, rows, 2 * cols), BF),
            pltpu.VMEM((xs, rows, 2 * cols), BF),
            pltpu.VMEM((xs, rows, (2 * reach + 1) * rows), F32),
            dma((13,)), dma((2,)), dma((2,)), dma((2,)), dma((2,)),
            dma((nx,)), dma((nx,)), dma((nx,)), dma((nx,)),
            dma((halves,)), dma((nx, halves)), dma((2, halves)), dma((2, nx, halves)),
            dma((slots // 2, halves)), dma((slots, halves)), dma((nx,)), dma((nx,)),
        ],
        compiler_params=pltpu.CompilerParams(
            collective_id=0, has_side_effects=True, vmem_limit_bytes=63 * 1024 * 1024),
    )(tile_ids, key_counts, grid_feat, mesh_feat, enc_query, enc_keyval, enc_out, proc_qkv,
      proc_out)


def solution(mesh):
    return jax.shard_map(
        functools.partial(local, mesh.shape["band"], mesh.shape["head"]),
        mesh=mesh,
        in_specs=(
            P(("band", "head"), None),
            P(("band", "head"), None),
            P(),
            P(),
            P(),
            P(None, None, "head"),
            P("head", None),
            P(("band", "head"), None),
            P(("band", "head")),
        ),
        out_specs=P(("band", "head"), None),
        check_vma=False,
    )
```

```python
import functools

import jax
import jax.numpy as jnp
from jax import lax
from jax.experimental import pallas as pl
from jax.experimental.pallas import tpu as pltpu
from jax.sharding import PartitionSpec as P

HEADS = 16
HALFW = 512
GT = 128
MT = 64
HALO_TILES = 2
BF = jnp.bfloat16
F32 = jnp.float32
MESH_ID = pl.DeviceIdType.MESH
NEG = -1e30
GROUP = 4


def dot(a, b):
    return jnp.dot(a, b, preferred_element_type=F32)


def dot_t(a, b):
    return lax.dot_general(a, b, (((1,), (1,)), ((), ())), preferred_element_type=F32)


def group_rows(q, count, width):
    lane = lax.broadcasted_iota(jnp.int32, q.shape, 1)
    zero = jnp.zeros_like(q)
    return jnp.concatenate(
        [jnp.where((lane >= i * width) & (lane < (i + 1) * width), q, zero)
         for i in range(count)], axis=0)


def group_merge(o, rows, count, width):
    lane = lax.broadcasted_iota(jnp.int32, (rows, count * width), 1)
    r = o[:rows]
    for i in range(1, count):
        r = jnp.where(lane < i * width, r, o[i * rows:(i + 1) * rows])
    return r


def softmax_rows(scores):
    top = jnp.max(scores, axis=-1, keepdims=True)
    weights = jnp.exp(scores - top)
    return (weights * (1.0 / jnp.sum(weights, axis=-1, keepdims=True))).astype(BF)


def kernel(
    nb, nh, tid, cnt, grid, feat_h, wquery_h, wkv_h, wenc_h, qkv_h, pout_h, out,
    g, halo, wkv, wquery, wenc, feat, kv, wq, wo, st, qs, att, qh, kp, vp, mine, got, bias,
    lsem, hs_send, hs_recv, w_send, w_recv, ox_send, ox_recv, op_send, op_recv,
    m_send, x_send, v_send, r_send, p_send, s_recv, a_send, a_recv,
):
    n = nb * nh
    band = lax.axis_index("band")
    head = lax.axis_index("head")
    d = band * nh + head
    core = lax.rem(head, 2)
    x = head // 2
    mate = head + 1 - 2 * core
    xs = nh // 2
    rows, dm = feat.shape
    tiles = grid.shape[0] // GT
    edge = HALO_TILES * GT
    cols = qkv_h.shape[2]
    slots = st.shape[0]
    reach = HALFW // rows
    hop = reach // 2
    halves = rows // MT
    head_size = dm // HEADS
    wide = GROUP * head_size
    scale = head_size ** (-0.5)

    def flat_id(f):
        return (f // nh, lax.rem(f, nh))

    def remote(src, dst, ss, rs, dev):
        return pltpu.make_async_remote_copy(
            src_ref=src, dst_ref=dst, send_sem=ss, recv_sem=rs, device_id=dev,
            device_id_type=MESH_ID)

    gchunk = g.shape[0] // 4
    wchunk = wkv.shape[1] // 4
    local = []
    for i in range(4):
        local.append(pltpu.make_async_copy(
            wkv_h.at[:, pl.ds(i * wchunk, wchunk)], wkv.at[:, pl.ds(i * wchunk, wchunk)],
            lsem.at[i]))
        local.append(pltpu.make_async_copy(
            grid.at[pl.ds(i * gchunk, gchunk)], g.at[pl.ds(i * gchunk, gchunk)], lsem.at[4 + i]))
    local.append(pltpu.make_async_copy(feat_h, feat, lsem.at[8]))
    local.append(pltpu.make_async_copy(wquery_h, wquery, lsem.at[9]))
    local.append(pltpu.make_async_copy(wenc_h, wenc, lsem.at[10]))
    local.append(pltpu.make_async_copy(qkv_h, wq.at[core], lsem.at[11]))

    def out_rows(src):
        return wo.at[pl.ds(pl.multiple_of(src * cols, cols), cols)]

    local.append(pltpu.make_async_copy(pout_h, out_rows(head), lsem.at[12]))
    for c in local:
        c.start()

    def same_core(k):
        return (band, lax.rem(head + 2 * k, nh))

    def same_core_src(h, k):
        return lax.rem(h - 2 * k + nh, nh)

    bar = pltpu.get_barrier_semaphore()
    expect = jnp.int32(0)
    for off in (-nh, -1, 1, nh):
        ok = (d + off >= 0) & (d + off < n)
        expect = expect + ok.astype(jnp.int32)

        @pl.when(ok)
        def _(off=off):
            pl.semaphore_signal(bar, inc=1, device_id=flat_id(d + off), device_id_type=MESH_ID)

    for k in range(1, xs):
        pl.semaphore_signal(bar, inc=1, device_id=same_core(k), device_id_type=MESH_ID)
    pl.semaphore_signal(bar, inc=1, device_id=(band, mate), device_id_type=MESH_ID)
    pl.semaphore_wait(bar, expect + xs)

    first, last = d == 0, d == n - 1
    up = remote(grid.at[pl.ds(grid.shape[0] - edge, edge)], halo.at[0], hs_send.at[0],
                hs_recv.at[0], flat_id(lax.rem(d + 1, n)))
    down = remote(grid.at[pl.ds(0, edge)], halo.at[1], hs_send.at[1], hs_recv.at[1],
                  flat_id(lax.rem(d + n - 1, n)))

    @pl.when(jnp.logical_not(last))
    def _():
        up.start()

    @pl.when(jnp.logical_not(first))
    def _():
        down.start()

    @pl.when(first)
    def _():
        halo[0] = jnp.zeros(halo.shape[1:], BF)

    @pl.when(last)
    def _():
        halo[1] = jnp.zeros(halo.shape[1:], BF)

    qkv_mate = remote(qkv_h, wq.at[core], w_send.at[0], w_recv.at[0], (band, mate))
    out_mate = remote(pout_h, out_rows(head), w_send.at[1], w_recv.at[1], (band, mate))

    def out_cross(k):
        return remote(pout_h, out_rows(head), ox_send.at[k - 1], ox_recv.at[k - 1], same_core(k))

    def out_pass(k):
        src = out_rows(same_core_src(head, k))
        return remote(src, src, op_send.at[k - 1], op_recv.at[k - 1], (band, mate))

    for k in range(1, xs):
        out_cross(k).start()
    qkv_mate.start()
    out_mate.start()

    below, above = band > 0, band < nb - 1
    for e in range(slots):
        if e < reach:
            ok = below
        elif e >= nh + reach:
            ok = above
        else:
            continue
        if e == 0:
            ok = ok & (core == 0)
        if e == slots - 1:
            ok = ok & (core == 1)

        @pl.when(jnp.logical_not(ok))
        def _(e=e):
            st[e] = jnp.zeros(st.shape[1:], BF)

    span = (2 * reach + 1) * rows
    brow = lax.broadcasted_iota(jnp.int32, (rows, span), 0)
    bcol = lax.broadcasted_iota(jnp.int32, (rows, span), 1)
    near = (bcol - HALFW - brow < HALFW) & (bcol - HALFW - brow > -HALFW)
    for q in range(xs):
        kpos = (band * nh + 2 * q + core - reach) * rows + bcol
        bias[q] = jnp.where(near & (kpos >= 0) & (kpos < n * rows), 0.0, NEG).astype(F32)

    for i in range(4):
        local[2 * i].wait()
    for i in range(4):
        local[2 * i + 1].wait()
        ct = gchunk // GT

        def col_step(j, _, i=i, ct=ct):
            cs = pl.ds(pl.multiple_of(j * wchunk, wchunk), wchunk)
            r = dot(g[pl.ds(i * gchunk, gchunk)], wkv[:, cs]).astype(BF)
            kv[pl.ds(HALO_TILES + i * ct, ct), :, cs] = r.reshape(ct, GT, wchunk)
            return 0

        lax.fori_loop(0, 4, col_step, 0)
    local[8].wait()
    local[9].wait()
    local[10].wait()
    qs[...] = (dot(feat[...], wquery[...]).astype(BF) * scale).astype(BF)

    @pl.when(jnp.logical_not(first))
    def _():
        up.wait_recv()

    @pl.when(jnp.logical_not(last))
    def _():
        down.wait_recv()

    def halo_step(j, _):
        cs = pl.ds(pl.multiple_of(j * wchunk, wchunk), wchunk)
        r = dot(halo[...].reshape(2 * edge, dm), wkv[:, cs]).astype(BF)
        r = r.reshape(2 * HALO_TILES, GT, wchunk)
        kv[pl.ds(0, HALO_TILES), :, cs] = r[:HALO_TILES]
        kv[pl.ds(HALO_TILES + tiles, HALO_TILES), :, cs] = r[HALO_TILES:]
        return 0

    lax.fori_loop(0, 4, halo_step, 0)

    own = head + reach
    to_above = above & (x >= xs - hop)
    to_below = below & (x < hop)

    def part(e, u):
        return st.at[e, pl.ds(u * MT, MT)]

    def state_mate(u):
        return remote(part(own, u), part(own, u), m_send.at[u], s_recv.at[own, u], (band, mate))

    def state_x(k, u):
        return remote(part(own, u), part(own, u), x_send.at[k - 1, u], s_recv.at[own, u],
                      same_core(k))

    def state_v(i, u):
        sign = 1 - 2 * i
        to = own - sign * nh
        to = jnp.clip(to, 0, slots - 1)
        dev = (jnp.clip(band + sign, 0, nb - 1), head)
        return remote(part(own, u), part(to, u), v_send.at[i, u], s_recv.at[to, u], dev)

    base = d * tiles - HALO_TILES
    lists = tid.shape[1]
    for m in range(halves):
        ids = [jnp.clip(tid[m, s] - base, 0, kv.shape[0] - 1) for s in range(lists)]
        valid = cnt[m]

        def group_step(j, _, m=m, ids=ids, valid=valid):
            cs = pl.ds(pl.multiple_of(j * wide, wide), wide)
            vs = pl.ds(pl.multiple_of(dm + j * wide, wide), wide)
            q2 = group_rows(qs[pl.ds(m * MT, MT), cs], GROUP, head_size)
            k2 = jnp.concatenate([kv[t, :, cs] for t in ids], axis=0)
            scores = dot_t(q2, k2)
            pos = lax.broadcasted_iota(jnp.int32, scores.shape, 1)
            w = softmax_rows(jnp.where(pos < valid, scores, NEG))
            v2 = jnp.concatenate([kv[t, :, vs] for t in ids], axis=0)
            att[pl.ds(m * MT, MT), cs] = group_merge(dot(w, v2), MT, GROUP, head_size).astype(BF)
            return 0

        lax.fori_loop(0, HEADS // GROUP, group_step, 0, unroll=2)
        ms = pl.ds(m * MT, MT)
        st[own, ms] = (feat[ms].astype(F32) + dot(att[ms], wenc[...])).astype(BF)
        for k in range(1, xs):
            state_x(k, m).start()
        for i, ok in enumerate((to_above, to_below)):
            @pl.when(ok)
            def _(i=i, m=m):
                state_v(i, m).start()
        state_mate(m).start()

    def arrived(e, u):
        remote(part(own, u), part(e, u), m_send.at[u], s_recv.at[e, u], (band, mate)).wait_recv()

    def slot_of(j):
        return 2 * j + core

    def mate_slot(j):
        return 2 * j + 1 - core

    def hand(j, u):
        e = slot_of(j)
        return remote(part(e, u), part(e, u), p_send.at[j, u], s_recv.at[e, u], (band, mate))

    def wanted(j):
        e = slot_of(j)
        return (e >= 1 - core) & (e <= slots - 1 - core)

    def relay(i, k, j, u):
        e = slot_of(j)
        return remote(part(e, u), part(e, u), r_send.at[i, k - 1, u], s_recv.at[e, u],
                      same_core(k))

    def project(j):
        def step(h, _):
            cs = pl.ds(pl.multiple_of(h * cols, cols), cols)
            rs = pl.ds(pl.multiple_of(j * 2 * rows, 2 * rows), 2 * rows)
            y = st[pl.ds(2 * j, 2)].reshape(2 * rows, dm)
            kp[rs, cs] = dot(y, wq[h, 1]).astype(BF)
            vp[rs, cs] = dot(y, wq[h, 2]).astype(BF)
            return 0

        lax.fori_loop(0, 2, step, 0)

    def from_mate(j):
        e = mate_slot(j)
        ok = (e >= core) & (e <= slots - 2 + core)
        if isinstance(j, int):
            if j < hop:
                ok = ok & below
            elif j >= xs + hop:
                ok = ok & above
        else:
            ok = ok & ((j >= hop) | below) & ((j < xs + hop) | above)

        @pl.when(ok)
        def _():
            for u in range(halves):
                arrived(e, u)

    def query(q):
        def step(h, _):
            cs = pl.ds(pl.multiple_of(h * cols, cols), cols)
            y = st[slot_of(q + hop)]
            qh[q, :, cs] = (dot(y, wq[h, 0]).astype(BF) * scale).astype(BF)
            return 0

        lax.fori_loop(0, 2, step, 0)

    local[11].wait()
    local[12].wait()
    remote(qkv_h, wq.at[1 - core], w_send.at[0], w_recv.at[0], (band, mate)).wait_recv()
    from_mate(x + hop)
    project(x + hop)

    others = [lax.rem(x + k, xs) for k in range(1, xs)]
    for q in others:
        for u in range(halves):
            arrived(slot_of(q + hop), u)
            hand(q + hop, u).start()

    direct = ((x + hop - xs, below & (x >= xs - hop)), (x + hop + xs, above & (x < hop)))

    def take_direct(u):
        for i, (j, ok) in enumerate(direct):
            @pl.when(ok)
            def _(i=i, j=j):
                arrived(slot_of(j), u)
                for k in range(1, xs):
                    relay(i, k, j, u).start()

            @pl.when(ok & wanted(j))
            def _(j=j):
                hand(j, u).start()

    take_direct(0)
    query(x)
    for u in range(1, halves):
        take_direct(u)
    for k in range(1, xs):
        src = out_rows(same_core_src(head, k))
        remote(pout_h, src, ox_send.at[k - 1], ox_recv.at[k - 1], same_core(k)).wait_recv()
        out_pass(k).start()
    for q in others:
        from_mate(q + hop)
        project(q + hop)
        query(q)

    far = []
    for j in range(hop):
        far.append((j, below & (x != xs - hop + j)))
    for j in range(hop):
        far.append((xs + hop + j, above & (x != j)))
    early = xs == hop == 2
    if early:
        for j in (x, x + xs + hop):
            from_mate(j)
            project(j)
    for u in range(halves):
        for j, ok in far:
            @pl.when(ok)
            def _(j=j, u=u):
                arrived(slot_of(j), u)

            @pl.when(ok & wanted(j))
            def _(j=j, u=u):
                hand(j, u).start()
    for j in (xs - 1 - x, slots // 2 - 1 - x) if early else [j for j, _ in far]:
        from_mate(j)
        project(j)

    half_cols = qh.shape[2]

    def att_to(k):
        return remote(mine.at[k], got.at[x], a_send.at[k - 1], a_recv.at[k - 1], same_core(k))

    def window(q, dst):
        rs = pl.ds(pl.multiple_of((2 * q + core) * rows, rows), span)

        def step(j, _):
            cs = pl.ds(pl.multiple_of(j * wide, wide), wide)
            q2 = group_rows(qh[q, :, cs], GROUP, head_size)
            b = bias[q]
            scores = dot_t(q2, kp[rs, cs]) + jnp.concatenate([b] * GROUP, axis=0)
            o = dot(softmax_rows(scores), vp[rs, cs])
            mine[dst, :, cs] = group_merge(o, rows, GROUP, head_size).astype(BF)
            return 0

        steps = half_cols // wide
        lax.fori_loop(0, steps, step, 0, unroll=min(steps, 2))

    for k in range(1, xs):
        window(lax.rem(x + k, xs), k)
        att_to(k).start()
    window(x, 0)

    def out_block(q):
        return wo[pl.ds(pl.multiple_of(q * half_cols, half_cols), half_cols)]

    remote(pout_h, out_rows(mate), w_send.at[1], w_recv.at[1], (band, mate)).wait_recv()
    for k in range(1, xs):
        src = out_rows(same_core_src(mate, k))
        remote(pout_h, src, op_send.at[k - 1], op_recv.at[k - 1], (band, mate)).wait_recv()
    total = st[own].astype(F32) + dot(mine[0], out_block(x))
    for k in range(1, xs):
        src = lax.rem(x - k + xs, xs)
        remote(mine.at[k], got.at[src], a_send.at[k - 1], a_recv.at[k - 1],
               same_core(k)).wait_recv()
        total = total + dot(got[src], out_block(src))
    out[...] = total.astype(BF)

    @pl.when(jnp.logical_not(last))
    def _():
        up.wait_send()

    @pl.when(jnp.logical_not(first))
    def _():
        down.wait_send()

    qkv_mate.wait_send()
    out_mate.wait_send()
    for k in range(1, xs):
        out_cross(k).wait_send()
        out_pass(k).wait_send()
        att_to(k).wait_send()
    for u in range(halves):
        state_mate(u).wait_send()
        for k in range(1, xs):
            state_x(k, u).wait_send()
        for i, ok in enumerate((to_above, to_below)):
            @pl.when(ok)
            def _(i=i, u=u):
                state_v(i, u).wait_send()
        for q in others:
            hand(q + hop, u).wait_send()
        for i, (j, ok) in enumerate(direct):
            @pl.when(ok)
            def _(i=i, j=j, u=u):
                for k in range(1, xs):
                    relay(i, k, j, u).wait_send()

            @pl.when(ok & wanted(j))
            def _(j=j, u=u):
                hand(j, u).wait_send()
        for j, ok in far:
            @pl.when(ok & wanted(j))
            def _(j=j, u=u):
                hand(j, u).wait_send()


def local(nb, nh, grid_feat, mesh_feat, enc_query, enc_keyval, enc_out, proc_qkv, proc_out,
          tile_ids, key_counts):
    rows, dm = mesh_feat.shape
    grows = grid_feat.shape[0]
    tiles = grows // GT + 2 * HALO_TILES
    reach = HALFW // rows
    slots = nh + 2 * reach
    cols = proc_qkv.shape[2]
    xs = nh // 2
    nx = max(xs - 1, 1)
    halves = rows // MT
    dma = pltpu.SemaphoreType.DMA
    any_spec = pl.BlockSpec(memory_space=pl.ANY)
    smem = pl.BlockSpec(memory_space=pltpu.SMEM)
    return pl.pallas_call(
        functools.partial(kernel, nb, nh),
        out_shape=jax.ShapeDtypeStruct((rows, dm), BF),
        in_specs=[smem, smem] + [any_spec] * 7,
        out_specs=pl.BlockSpec(memory_space=pltpu.VMEM),
        scratch_shapes=[
            pltpu.VMEM((grows, dm), BF),
            pltpu.VMEM((2, HALO_TILES * GT, dm), BF),
            pltpu.VMEM(enc_keyval.shape, BF),
            pltpu.VMEM(enc_query.shape, BF),
            pltpu.VMEM(enc_out.shape, BF),
            pltpu.VMEM((rows, dm), BF),
            pltpu.VMEM((tiles, GT, 2 * dm), BF),
            pltpu.VMEM((2, 3, dm, cols), BF),
            pltpu.VMEM((nh * cols, dm), BF),
            pltpu.VMEM((slots, rows, dm), BF),
            pltpu.VMEM((rows, dm), BF),
            pltpu.VMEM((rows, dm), BF),
            pltpu.VMEM((xs, rows, 2 * cols), BF),
            pltpu.VMEM((slots * rows, 2 * cols), BF),
            pltpu.VMEM((slots * rows, 2 * cols), BF),
            pltpu.VMEM((xs, rows, 2 * cols), BF),
            pltpu.VMEM((xs, rows, 2 * cols), BF),
            pltpu.VMEM((xs, rows, (2 * reach + 1) * rows), F32),
            dma((13,)), dma((2,)), dma((2,)), dma((2,)), dma((2,)),
            dma((nx,)), dma((nx,)), dma((nx,)), dma((nx,)),
            dma((halves,)), dma((nx, halves)), dma((2, halves)), dma((2, nx, halves)),
            dma((slots // 2, halves)), dma((slots, halves)), dma((nx,)), dma((nx,)),
        ],
        compiler_params=pltpu.CompilerParams(
            collective_id=0, has_side_effects=True, vmem_limit_bytes=63 * 1024 * 1024),
    )(tile_ids, key_counts, grid_feat, mesh_feat, enc_query, enc_keyval, enc_out, proc_qkv,
      proc_out)


def solution(mesh):
    return jax.shard_map(
        functools.partial(local, mesh.shape["band"], mesh.shape["head"]),
        mesh=mesh,
        in_specs=(
            P(("band", "head"), None),
            P(("band", "head"), None),
            P(),
            P(),
            P(),
            P(None, None, "head"),
            P("head", None),
            P(("band", "head"), None),
            P(("band", "head")),
        ),
        out_specs=P(("band", "head"), None),
        check_vma=False,
    )
```
